32 devices in a mesh: groups: 2 (over x), req: 8 (over z, y), head: 2 (over core).
Axes of the slice: x: 2, y: 2, z: 4, core: 2. Of those that a mesh axis runs over, the one named last changes fastest.
Arguments:
- queries: bfloat16 [2048, 32, 128], P(('groups', 'req'), 'head'), parts along dimension 0, may hold values from -100 to 100
- new_keys: bfloat16 [2048, 2, 128], P(('groups', 'req'), 'head'), parts along dimension 0, may hold values from -4.5 to 4.5
- new_values: bfloat16 [2048, 2, 128], P(('groups', 'req'), 'head'), parts along dimension 0, may hold values from -6 to 6
- cluster_kv: bfloat16 [1024, 2, 2, 128, 128], P(('groups', 'req'), 'head'), parts along dimension 0, may hold values from -6 to 6
- cluster_len: int32 [32], P('groups'), parts along dimension 0, may hold values from 1 to 4096, 40960 in all
- piece_slot: int32 [32, 32], P('groups'), parts along dimension 0, may hold values from 0 to 511, as said below
- cluster_ids: int32 [16, 2, 2], P('groups', 'head'), parts along dimension 0, may hold values from 0 to 15, all different within a row
- w_out: bfloat16 [4096, 4096], P('head', 'req'), may hold values from -0.09375 to 0.09375
Outputs:
- projected: bfloat16 [2048, 4096], P(('groups', 'req', 'head')), parts along dimension 0
The draws below stay inside these ranges and needn't reach their ends.
There are 2 independent parts, one for each index of `groups`. The reference program is written for one: setup_inputs(seed, part) draws one part's arguments, and reference() takes and returns one part's arrays. A program takes and returns all parts, laid end to end along the dimension named above; an argument that names none is the same for every part. Nothing has to cross between parts.
Inputs may be any that keep to these rules, and one draw needn't show every extreme that they name: `cluster_ids`: for each request and KV head, 2 distinct cluster numbers. A permutation of the slots: piece p of cluster c lies in slot piece_slot[c, p], stored on index slot // 64 of req, and every cluster has exactly 4 of its pieces on every index of req.
All inputs are finite; a program needn't handle non-finite values.
Results may differ from the reference program's by a relative error of at most 0.0052.
Values may be sent and summed in bfloat16 or wider, within the bound.
A program may use at most 128 MiB of HBM per device.

```python
import math
import jax
import jax.numpy as jnp
import numpy as np
from jax import lax

D = 4096
HD = 128
QH = 32
KVH = 2
PIECE = 128
PCS = 32
NCL_DEV = 2
SEL = 2
TOK = 128
CL = 4096
NCL = 16
N_REQ = 8


def shared_keys(key):
    normal_keys = jax.random.normal(jax.random.fold_in(key, 7), (N_REQ * TOK, KVH, HD), jnp.float32)
    return jnp.clip(normal_keys, -4.5, 4.5)


def draw_new_keys(key, part):
    return shared_keys(key).astype(jnp.bfloat16)


def draw_queries(key, part):
    first_key = jax.random.fold_in(key, 13)
    second_key = jax.random.fold_in(key, 17)
    shape = (N_REQ * TOK, QH, HD)
    base = jax.random.normal(first_key, shape, jnp.float32)
    scales = jnp.exp(jax.random.uniform(second_key, (N_REQ * TOK, QH, 1), jnp.float32, -0.7, 1.1))
    result = base * scales
    return jnp.clip(result, -100.0, 100.0).astype(jnp.bfloat16)


def draw_piece_slot(key, part):
    per_peer = PCS // N_REQ
    held_slots = NCL_DEV * PCS
    first_scores = jax.random.randint(jax.random.fold_in(key, 41), (NCL, PCS), 0, 1 << 20) * PCS + jnp.arange(PCS, dtype=jnp.int32)[None, :]
    position = jnp.argsort(first_scores, axis=1).astype(jnp.int32)
    owner_index = position % N_REQ
    within = position // N_REQ
    second_scores = jax.random.randint(jax.random.fold_in(key, 42), (N_REQ, held_slots), 0, 1 << 20) * held_slots + jnp.arange(held_slots, dtype=jnp.int32)[None, :]
    device_perm = jnp.argsort(second_scores, axis=1).astype(jnp.int32)
    entry = jnp.arange(NCL, dtype=jnp.int32)[:, None] * per_peer + within
    local_slot = device_perm[owner_index, entry]
    return (owner_index * held_slots + local_slot).astype(jnp.int32)


def block_levels(key, extent, pieces, least, high):
    factor_of, own = 1.0, jax.random.fold_in(key, 6)
    for dim, parts in pieces:
        draws = jnp.exp(jax.random.uniform(jax.random.fold_in(own, dim), (parts,), jnp.float32, least / len(pieces), high / len(pieces)))
        factor_of = factor_of * jnp.repeat(draws, extent[dim] // parts).reshape([-1 if axis == dim else 1 for axis in range(len(extent))])
    return factor_of


def different_ones(stream_key, rows, count, top, lift):
    sequence = jax.random.permutation(jax.random.fold_in(stream_key, 1), count)
    boost = sequence
    for power in range(3):
        boost = boost * boost // count
    boost = boost * lift // count
    lots = jax.random.randint(jax.random.fold_in(stream_key, 2), (rows, count), 0, 4096) + boost
    fixed_rows = jax.random.permutation(jax.random.fold_in(stream_key, 3), rows)[jnp.arange(count) % rows]
    lots = jnp.where(jnp.arange(rows)[:, None] == fixed_rows[None, :], 1 << 14, lots)
    priority = lots * count + jnp.arange(count)
    return lax.top_k(priority.astype(jnp.int32), top)[1].astype(jnp.int32)


def length_profile(number_of, total, reach, skew):
    weights = [(1 << 20) // math.isqrt(standing ** skew) + 1 for standing in range(2, number_of + 1)]
    spare, counts = total - reach - (number_of - 1), [1] * (number_of - 1)
    while spare > 0:
        candidates = [i for i in range(number_of - 1) if counts[i] < reach]
        whole, remaining = sum([weights[i] for i in candidates]), spare
        for i in candidates:
            extra = min(reach - counts[i], max(1, remaining * weights[i] // whole), spare)
            counts[i] = counts[i] + extra
            spare = spare - extra
    return np.array([reach] + counts)


def ragged_sizes(key, count, total, limit, lean):
    if count == 2:
        one = jax.random.randint(key, (), max(1, total - limit), min(limit, total - 1) + 1)
        return jnp.stack([one, total - one])
    sizes = jnp.asarray(length_profile(count, total, limit, lean), jnp.int32)
    twos = (count - 1) // 2
    source_of, receiver = sizes[1:1 + 2 * twos:2], sizes[2:2 + 2 * twos:2]
    margin = jnp.minimum(source_of - 1, limit - receiver)
    passed = jax.random.randint(jax.random.fold_in(key, 1), (twos,), 0, 1 << 20) % (margin + 1)
    sizes = sizes.at[1:1 + 2 * twos:2].set(source_of - passed).at[2:2 + 2 * twos:2].set(receiver + passed)
    return sizes[jax.random.permutation(jax.random.fold_in(key, 2), count)]


def bell_draw(rng, extent, spread, reach, split=(), held_as=jnp.bfloat16):
    array = jax.random.normal(rng, extent, jnp.float32) * spread
    if len(split) > 0:
        array = block_levels(rng, extent, split, -0.22, 0.18) * array
    return jnp.clip(array, min=-reach, max=reach).astype(held_as)


def setup_inputs(seed: int = 0, part: int = 0) -> dict:
    streams_of = jax.random.split(jax.random.key(seed), 9)
    part_splits = jax.random.split(jax.random.fold_in(streams_of[8], part), 9)
    queries = draw_queries(jax.random.fold_in(jax.random.fold_in(streams_of[8], part), 71), part)
    new_keys = draw_new_keys(jax.random.fold_in(jax.random.fold_in(streams_of[8], part), 71), part)
    new_values = bell_draw(part_splits[2], (N_REQ * TOK, KVH, HD), 1.0, 6.0, ((0, 8), (1, 2)))
    cluster_kv = bell_draw(part_splits[3], (NCL * PCS, KVH, 2, PIECE, HD), 1.0, 6.0, ((0, 8), (1, 2)))
    cluster_len = ragged_sizes(part_splits[4], NCL, NCL * CL * 5 // 8, CL, 1).astype(jnp.int32)
    piece_slot = draw_piece_slot(jax.random.fold_in(jax.random.fold_in(streams_of[8], part), 71), part)
    cluster_ids = different_ones(part_splits[6], N_REQ * KVH, NCL, SEL, 1024).reshape((N_REQ, KVH, SEL))
    w_out = bell_draw(streams_of[7], (QH * HD, D), (QH * HD) ** -0.5, 0.09375, ((0, 2), (1, 8)))
    return {"queries": queries, "new_keys": new_keys, "new_values": new_values, "cluster_kv": cluster_kv, "cluster_len": cluster_len, "piece_slot": piece_slot, "cluster_ids": cluster_ids, "w_out": w_out}


def reference(queries, new_keys, new_values, cluster_kv, cluster_len, piece_slot, cluster_ids, w_out):
    group_size = QH // KVH
    scale_factor = HD ** -0.5
    position = jnp.arange(TOK, dtype=jnp.int32)
    causal = position[:, None] >= position[None, :]
    key_offset = (jnp.arange(PCS, dtype=jnp.int32)[:, None] * PIECE + jnp.arange(PIECE, dtype=jnp.int32)[None, :]).reshape(CL)

    def per_request(request):
        start_row = (request * TOK).astype(jnp.int32)
        query_rows = lax.dynamic_slice_in_dim(queries, start_row, TOK, 0)
        key_rows = lax.dynamic_slice_in_dim(new_keys, start_row, TOK, 0)
        value_rows = lax.dynamic_slice_in_dim(new_values, start_row, TOK, 0)
        plan_row = lax.dynamic_index_in_dim(cluster_ids, request, 0, keepdims=False)
        outputs = []
        for group_index in range(KVH):
            chosen = plan_row[group_index]
            slot_rows = piece_slot[chosen].reshape(SEL * PCS)
            picked = cluster_kv[slot_rows, group_index]
            lengths = cluster_len[chosen]
            valid_keys = (key_offset[None, :] < lengths[:, None]).reshape(SEL * CL)
            cached_keys = picked[:, 0].reshape(SEL * CL, HD).astype(jnp.float32)
            cached_values = picked[:, 1].reshape(SEL * CL, HD).astype(jnp.float32)
            own_keys = key_rows[:, group_index].astype(jnp.float32)
            own_values = value_rows[:, group_index].astype(jnp.float32)
            query_group = query_rows[:, group_index * group_size:(group_index + 1) * group_size].astype(jnp.float32)
            cached_scores = jnp.einsum("thd,kd->htk", query_group, cached_keys) * scale_factor
            cached_scores = jnp.where(valid_keys[None, None, :], cached_scores, -jnp.inf)
            own_scores = jnp.einsum("thd,ud->htu", query_group, own_keys) * scale_factor
            own_scores = jnp.where(causal[None], own_scores, -jnp.inf)
            row_top = jnp.maximum(jnp.max(cached_scores, axis=2), jnp.max(own_scores, axis=2))
            cached_weights = jnp.exp(cached_scores - row_top[:, :, None])
            own_weights = jnp.exp(own_scores - row_top[:, :, None])
            row_total = jnp.sum(cached_weights, axis=2) + jnp.sum(own_weights, axis=2)
            cached_low = cached_weights.astype(jnp.bfloat16).astype(jnp.float32)
            own_low = own_weights.astype(jnp.bfloat16).astype(jnp.float32)
            mixed_sum = jnp.einsum("htk,kd->htd", cached_low, cached_values) + jnp.einsum("htu,ud->htd", own_low, own_values)
            result = (mixed_sum / row_total[:, :, None]).astype(jnp.bfloat16)
            outputs.append(jnp.transpose(result, (1, 0, 2)))
        return jnp.concatenate(outputs, axis=1).reshape(TOK, QH * HD)

    attended = lax.map(per_request, jnp.arange(N_REQ, dtype=jnp.int32)).reshape(N_REQ * TOK, QH * HD)
    return jnp.dot(attended, w_out, preferred_element_type=jnp.float32).astype(jnp.bfloat16)
```

```python
import functools

import jax
import jax.numpy as jnp
from jax import lax
from jax.experimental import pallas as pl
from jax.experimental.pallas import tpu as pltpu
from jax.sharding import PartitionSpec as P

MESH = pl.DeviceIdType.MESH
NEG = -1e30
LOG2E = 1.4426950408889634


def pick_kernel(peers, ids_ref, slot_ref, len_ref, kv_ref, send_ref, lim_ref, pick, count, sem):
    me = lax.axis_index("req")
    held, _, _, piece_keys, _ = kv_ref.shape
    sel = ids_ref.shape[1]
    pieces = slot_ref.shape[1]
    per = pieces // peers
    base = me * held

    @pl.loop(0, peers)
    def _(r):
        for s in range(sel):
            c = ids_ref[r, s]
            n = jnp.int32(0)
            for p in range(pieces):
                loc = slot_ref[c, p] - base
                pick[n] = loc
                n = n + ((loc >= 0) & (loc < held)).astype(jnp.int32)
            for j in range(per):
                pltpu.make_async_copy(kv_ref.at[pick[j], 0], send_ref.at[r, s * per + j], sem).start()

    for s in range(sel):
        c = ids_ref[me, s]
        fill = len_ref[c]
        for o in range(peers):
            count[o] = 0
        for p in range(pieces):
            o = slot_ref[c, p] // held
            j = count[o]
            lim_ref[o, s * per + j] = fill - p * piece_keys
            count[o] = j + 1
    pltpu.make_async_copy(send_ref, send_ref, sem).wait()


def attend_kernel(peers, heads, lim_ref, send_ref, q_ref, k_ref, v_ref, out_ref,
                  recv, qt, vt, top, total, acc, send_sem, recv_sem):
    me = lax.axis_index("req")
    tok = q_ref.shape[0]
    hd = k_ref.shape[1]
    count = send_ref.shape[1]
    piece_keys = send_ref.shape[3]
    rows = heads * tok
    block = min(256, rows)
    factor = hd ** (-0.5) * LOG2E

    barrier = pltpu.get_barrier_semaphore()
    for k in range(1, peers):
        pl.semaphore_signal(barrier, inc=1, device_id={"req": lax.rem(me + k, peers)}, device_id_type=MESH)
    pl.semaphore_wait(barrier, peers - 1)

    def peer_of(i):
        off = jnp.where(i % 2 == 1, (i + 1) // 2, peers - i // 2)
        return lax.rem(me + off, peers)

    def copy_to(peer):
        return pltpu.make_async_remote_copy(
            src_ref=send_ref.at[peer], dst_ref=recv.at[me],
            send_sem=send_sem.at[peer], recv_sem=recv_sem.at[me],
            device_id={"req": peer}, device_id_type=MESH)

    def copy_from(peer):
        return pltpu.make_async_remote_copy(
            src_ref=send_ref.at[peer], dst_ref=recv.at[peer],
            send_sem=send_sem.at[peer], recv_sem=recv_sem.at[peer],
            device_id={"req": peer}, device_id_type=MESH)

    @pl.loop(1, peers)
    def _(i):
        copy_to(peer_of(peers - i)).start()

    for h in range(heads):
        cols = slice(h * hd, (h + 1) * hd)
        qt[:, h * tok:(h + 1) * tok] = q_ref[:, cols].T
    own_vt = v_ref[...].T

    @pl.loop(0, rows // block)
    def _(b):
        cols = pl.ds(pl.multiple_of(b * block, block), block)
        s = jnp.dot(k_ref[...], qt[:, cols], preferred_element_type=jnp.float32)
        u = lax.broadcasted_iota(jnp.int32, s.shape, 0)
        t = lax.broadcasted_iota(jnp.int32, s.shape, 1) % tok
        s = jnp.where(u <= t, s, NEG)
        m = jnp.max(s, axis=0, keepdims=True)
        w = jnp.exp2((s - m) * factor)
        top[:, cols] = m
        total[:, cols] = jnp.sum(w, axis=0, keepdims=True)
        acc[:, cols] = jnp.dot(own_vt, w.astype(jnp.bfloat16), preferred_element_type=jnp.float32)

    def attend(src_ref, peer):
        for i in range(count):
            vt[:, i * piece_keys:(i + 1) * piece_keys] = src_ref[peer, i, 1].T

        @pl.loop(0, rows // block)
        def _(b):
            cols = pl.ds(pl.multiple_of(b * block, block), block)
            q = qt[:, cols]
            key = lax.broadcasted_iota(jnp.int32, (piece_keys, block), 0)
            m_old = top[:, cols]
            m = m_old
            scores = []
            for i in range(count):
                s = jnp.dot(src_ref[peer, i, 0], q, preferred_element_type=jnp.float32)
                s = jnp.where(key < lim_ref[peer, i], s, NEG)
                m = jnp.maximum(m, jnp.max(s, axis=0, keepdims=True))
                scores.append(s)
            keep = jnp.exp2((m_old - m) * factor)
            sums = total[:, cols] * keep
            low = []
            for s in scores:
                w = jnp.exp2((s - m) * factor)
                sums = sums + jnp.sum(w, axis=0, keepdims=True)
                low.append(w.astype(jnp.bfloat16))
            mixed = jnp.dot(vt[...], jnp.concatenate(low, axis=0), preferred_element_type=jnp.float32)
            top[:, cols] = m
            total[:, cols] = sums
            acc[:, cols] = acc[:, cols] * keep + mixed

    attend(send_ref, me)

    @pl.loop(1, peers)
    def _(i):
        peer = peer_of(i)
        copy_from(peer).wait_recv()
        attend(recv, peer)

    for h in range(heads):
        rows_h = slice(h * tok, (h + 1) * tok)
        o = acc[:, rows_h] / total[:, rows_h]
        out_ref[:, h * hd:(h + 1) * hd] = o.T.astype(out_ref.dtype)

    @pl.loop(1, peers)
    def _(i):
        copy_to(peer_of(i)).wait_send()


def local(queries, new_keys, new_values, cluster_kv, cluster_len, piece_slot, cluster_ids, w_out):
    peers = lax.axis_size("req")
    tok, heads, hd = queries.shape
    piece_keys = cluster_kv.shape[3]
    pieces = piece_slot.shape[1]
    sel = cluster_ids.shape[2]
    count = sel * (pieces // peers)
    vmem = pl.BlockSpec(memory_space=pltpu.VMEM)
    smem = pl.BlockSpec(memory_space=pltpu.SMEM)
    send, lim = pl.pallas_call(
        functools.partial(pick_kernel, peers),
        out_shape=(
            jax.ShapeDtypeStruct((peers, count, 2, piece_keys, hd), cluster_kv.dtype),
            jax.ShapeDtypeStruct((peers, count), jnp.int32),
        ),
        in_specs=[smem, smem, smem, pl.BlockSpec(memory_space=pl.ANY)],
        out_specs=(vmem, smem),
        scratch_shapes=[
            pltpu.SMEM((pieces + 1,), jnp.int32),
            pltpu.SMEM((peers,), jnp.int32),
            pltpu.SemaphoreType.DMA,
        ],
        name="pick",
    )(cluster_ids[:, 0, :], piece_slot, cluster_len, cluster_kv)
    rows = heads * tok
    attended = pl.pallas_call(
        functools.partial(attend_kernel, peers, heads),
        out_shape=jax.ShapeDtypeStruct((tok, heads * hd), jnp.bfloat16),
        in_specs=[smem, vmem, vmem, vmem, vmem],
        out_specs=vmem,
        scratch_shapes=[
            pltpu.VMEM((peers, count, 2, piece_keys, hd), cluster_kv.dtype),
            pltpu.VMEM((hd, rows), jnp.bfloat16),
            pltpu.VMEM((hd, count * piece_keys), jnp.bfloat16),
            pltpu.VMEM((1, rows), jnp.float32),
            pltpu.VMEM((1, rows), jnp.float32),
            pltpu.VMEM((hd, rows), jnp.float32),
            pltpu.SemaphoreType.DMA((peers,)),
            pltpu.SemaphoreType.DMA((peers,)),
        ],
        compiler_params=pltpu.CompilerParams(
            collective_id=0, has_side_effects=True, vmem_limit_bytes=40 * 2**20),
        name="attend",
    )(lim, send, queries.reshape(tok, heads * hd), new_keys[:, 0], new_values[:, 0])
    gathered = lax.all_gather(attended, "req", axis=0, tiled=True)
    terms = jnp.dot(gathered, w_out, preferred_element_type=jnp.float32)
    columns = w_out.shape[1]
    terms = terms.reshape(peers, tok, columns)
    summed = lax.psum_scatter(terms, "head", scatter_dimension=1, tiled=True).astype(jnp.bfloat16)
    mine = lax.all_to_all(summed, "req", split_axis=0, concat_axis=0, tiled=True)
    return jnp.transpose(mine, (1, 0, 2)).reshape(mine.shape[1], peers * columns)


def solution(mesh):
    return jax.shard_map(
        local,
        mesh=mesh,
        in_specs=(
            P(("groups", "req"), "head", None),
            P(("groups", "req"), "head", None),
            P(("groups", "req"), "head", None),
            P(("groups", "req"), "head", None, None, None),
            P("groups"),
            P("groups", None),
            P("groups", "head", None),
            P("head", "req"),
        ),
        out_specs=P(("groups", "req", "head"), None),
        check_vma=False,
    )
```

```python
import functools

import jax
import jax.numpy as jnp
from jax import lax
from jax.experimental import pallas as pl
from jax.experimental.pallas import tpu as pltpu
from jax.sharding import PartitionSpec as P

MESH = pl.DeviceIdType.MESH
NEG = -1e30
LOG2E = 1.4426950408889634


def pick_kernel(peers, ids_ref, slot_ref, len_ref, kv_ref, send_ref, lim_ref, pick, count, sem):
    me = lax.axis_index("req")
    held, _, _, piece_keys, _ = kv_ref.shape
    sel = ids_ref.shape[1]
    pieces = slot_ref.shape[1]
    per = pieces // peers
    base = me * held

    @pl.loop(0, peers)
    def _(r):
        for s in range(sel):
            c = ids_ref[r, s]
            n = jnp.int32(0)
            for p in range(pieces):
                loc = slot_ref[c, p] - base
                pick[n] = loc
                n = n + ((loc >= 0) & (loc < held)).astype(jnp.int32)
            for j in range(per):
                pltpu.make_async_copy(kv_ref.at[pick[j], 0], send_ref.at[r, s * per + j], sem).start()

    for s in range(sel):
        c = ids_ref[me, s]
        fill = len_ref[c]
        for o in range(peers):
            count[o] = 0
        for p in range(pieces):
            o = slot_ref[c, p] // held
            j = count[o]
            lim_ref[o, s * per + j] = fill - p * piece_keys
            count[o] = j + 1
    pltpu.make_async_copy(send_ref, send_ref, sem).wait()


def attend_kernel(peers, heads, lim_ref, send_ref, q_ref, k_ref, v_ref, w_ref, out_ref, w_pair_ref,
                  recv, qt, vt, top, total, acc, send_sem, recv_sem, w_sem):
    me = lax.axis_index("req")
    tok = q_ref.shape[0]
    hd = k_ref.shape[1]
    count = send_ref.shape[1]
    piece_keys = send_ref.shape[3]
    rows = heads * tok
    block = min(256, rows)
    factor = hd ** (-0.5) * LOG2E

    barrier = pltpu.get_barrier_semaphore()
    for k in range(1, peers):
        pl.semaphore_signal(barrier, inc=1, device_id={"req": lax.rem(me + k, peers)}, device_id_type=MESH)
    pl.semaphore_wait(barrier, peers - 1)

    def peer_of(i):
        off = jnp.where(i % 2 == 1, (i + 1) // 2, peers - i // 2)
        return lax.rem(me + off, peers)

    def copy_to(peer):
        return pltpu.make_async_remote_copy(
            src_ref=send_ref.at[peer], dst_ref=recv.at[me],
            send_sem=send_sem.at[peer], recv_sem=recv_sem.at[me],
            device_id={"req": peer}, device_id_type=MESH)

    def copy_from(peer):
        return pltpu.make_async_remote_copy(
            src_ref=send_ref.at[peer], dst_ref=recv.at[peer],
            send_sem=send_sem.at[peer], recv_sem=recv_sem.at[peer],
            device_id={"req": peer}, device_id_type=MESH)

    @pl.loop(1, peers)
    def _(i):
        copy_to(peer_of(peers - i)).start()

    pair_copy = pltpu.make_async_remote_copy(
        src_ref=w_ref, dst_ref=w_pair_ref, send_sem=w_sem.at[0], recv_sem=w_sem.at[1],
        device_id={"req": me + 1 - 2 * (me % 2)}, device_id_type=MESH)
    pair_copy.start()

    for h in range(heads):
        cols = slice(h * hd, (h + 1) * hd)
        qt[:, h * tok:(h + 1) * tok] = q_ref[:, cols].T
    own_vt = v_ref[...].T

    @pl.loop(0, rows // block)
    def _(b):
        cols = pl.ds(pl.multiple_of(b * block, block), block)
        s = jnp.dot(k_ref[...], qt[:, cols], preferred_element_type=jnp.float32)
        u = lax.broadcasted_iota(jnp.int32, s.shape, 0)
        t = lax.broadcasted_iota(jnp.int32, s.shape, 1) % tok
        s = jnp.where(u <= t, s, NEG)
        m = jnp.max(s, axis=0, keepdims=True)
        w = jnp.exp2((s - m) * factor)
        top[:, cols] = m
        total[:, cols] = jnp.sum(w, axis=0, keepdims=True)
        acc[:, cols] = jnp.dot(own_vt, w.astype(jnp.bfloat16), preferred_element_type=jnp.float32)

    def attend(src_ref, peer):
        for i in range(count):
            vt[:, i * piece_keys:(i + 1) * piece_keys] = src_ref[peer, i, 1].T

        @pl.loop(0, rows // block)
        def _(b):
            cols = pl.ds(pl.multiple_of(b * block, block), block)
            q = qt[:, cols]
            key = lax.broadcasted_iota(jnp.int32, (piece_keys, block), 0)
            m_old = top[:, cols]
            m = m_old
            scores = []
            for i in range(count):
                s = jnp.dot(src_ref[peer, i, 0], q, preferred_element_type=jnp.float32)
                s = jnp.where(key < lim_ref[peer, i], s, NEG)
                m = jnp.maximum(m, jnp.max(s, axis=0, keepdims=True))
                scores.append(s)
            keep = jnp.exp2((m_old - m) * factor)
            sums = total[:, cols] * keep
            low = []
            for s in scores:
                w = jnp.exp2((s - m) * factor)
                sums = sums + jnp.sum(w, axis=0, keepdims=True)
                low.append(w.astype(jnp.bfloat16))
            mixed = jnp.dot(vt[...], jnp.concatenate(low, axis=0), preferred_element_type=jnp.float32)
            top[:, cols] = m
            total[:, cols] = sums
            acc[:, cols] = acc[:, cols] * keep + mixed

    attend(send_ref, me)

    @pl.loop(1, peers)
    def _(i):
        peer = peer_of(i)
        copy_from(peer).wait_recv()
        attend(recv, peer)

    for h in range(heads):
        rows_h = slice(h * tok, (h + 1) * tok)
        o = acc[:, rows_h] / total[:, rows_h]
        out_ref[:, h * hd:(h + 1) * hd] = o.T.astype(out_ref.dtype)

    @pl.loop(1, peers)
    def _(i):
        copy_to(peer_of(i)).wait_send()

    pair_copy.wait()


def project_kernel(far, att_ref, w_ref, w_pair_ref, out_ref,
                   full, wv, part, got, low, load_sem, send_sem, recv_sem,
                   part_send, part_recv, out_send, out_recv):
    me = lax.axis_index("req")
    head = lax.axis_index("head")
    hi, lo = me // 2, me % 2
    half = out_ref.shape[0]
    columns = w_ref.shape[1]
    wide = 2 * columns

    def at(z):
        return {"req": z * 2 + lo}

    load_own = pltpu.make_async_copy(att_ref, full.at[hi], load_sem.at[0])
    load_w = pltpu.make_async_copy(w_ref, wv.at[lo], load_sem.at[1])
    load_pair = pltpu.make_async_copy(w_pair_ref, wv.at[1 - lo], load_sem.at[2])
    load_own.start()
    load_w.start()
    load_pair.start()

    barrier = pltpu.get_barrier_semaphore()
    for k in range(1, far):
        pl.semaphore_signal(barrier, inc=1, device_id=at(lax.rem(hi + k, far)), device_id_type=MESH)
    pl.semaphore_signal(barrier, inc=1, device_id={"head": 1 - head}, device_id_type=MESH)
    pl.semaphore_wait(barrier, far)

    def block_copy(z, to, way):
        return pltpu.make_async_remote_copy(
            src_ref=full.at[z], dst_ref=full.at[z], send_sem=send_sem.at[way, z],
            recv_sem=recv_sem.at[z], device_id=at(to), device_id_type=MESH)

    def part_copy(z):
        return pltpu.make_async_remote_copy(
            src_ref=part.at[z, 1 - head], dst_ref=got.at[z], send_sem=part_send.at[z],
            recv_sem=part_recv.at[z], device_id={"head": 1 - head}, device_id_type=MESH)

    def out_copy(z, owner):
        return pltpu.make_async_remote_copy(
            src_ref=low.at[z], dst_ref=out_ref.at[:, pl.ds(pl.multiple_of(owner * wide, wide), wide)],
            send_sem=out_send.at[z], recv_sem=out_recv.at[owner], device_id=at(z), device_id_type=MESH)

    def compute(z):
        @pl.loop(0, 2)
        def _(j):
            cols = pl.ds(pl.multiple_of(j * columns, columns), columns)
            terms = jnp.dot(full[z], wv[j], preferred_element_type=jnp.float32)
            part[z, 0, :, cols] = terms[:half]
            part[z, 1, :, cols] = terms[half:]
        part_copy(z).start()

    def finish(z):
        part_copy(z).wait_recv()
        rows = (part[z, head] + got[z]).astype(out_ref.dtype)

        @pl.when(z == hi)
        def _():
            out_ref[:, pl.ds(pl.multiple_of(hi * wide, wide), wide)] = rows

        @pl.when(z != hi)
        def _():
            low[z] = rows
            out_copy(z, hi).start()

    load_own.wait()

    @pl.when(hi < far - 1)
    def _():
        block_copy(hi, hi + 1, 0).start()

    @pl.when(hi > 0)
    def _():
        block_copy(hi, hi - 1, 1).start()

    load_w.wait()
    load_pair.wait()
    compute(hi)

    @pl.loop(1, far + 1)
    def _(d):
        @pl.when((hi - d >= 0) & (d < far))
        def _():
            block_copy(hi - d, hi, 0).wait_recv()

            @pl.when(hi < far - 1)
            def _():
                block_copy(hi - d, hi + 1, 0).start()

        @pl.when(hi + d < far)
        def _():
            block_copy(hi + d, hi, 1).wait_recv()

            @pl.when(hi > 0)
            def _():
                block_copy(hi + d, hi - 1, 1).start()

        @pl.loop(0, 2)
        def _(side):
            z = hi + d * (2 * side - 1)

            @pl.when((z >= 0) & (z < far))
            def _():
                compute(z)

        @pl.loop(0, 2)
        def _(side):
            z = hi + (d - 1) * (2 * side - 1)

            @pl.when((z >= 0) & (z < far) & ((d > 1) | (side == 0)))
            def _():
                finish(z)

    @pl.loop(0, far)
    def _(z):
        @pl.when((z <= hi) & (hi < far - 1))
        def _():
            block_copy(z, hi + 1, 0).wait_send()

        @pl.when((z >= hi) & (hi > 0))
        def _():
            block_copy(z, hi - 1, 1).wait_send()

        part_copy(z).wait_send()

        @pl.when(z != hi)
        def _():
            out_copy(z, hi).wait_send()
            out_copy(z, z).wait_recv()


def local(queries, new_keys, new_values, cluster_kv, cluster_len, piece_slot, cluster_ids, w_out):
    peers = lax.axis_size("req")
    tok, heads, hd = queries.shape
    piece_keys = cluster_kv.shape[3]
    pieces = piece_slot.shape[1]
    sel = cluster_ids.shape[2]
    count = sel * (pieces // peers)
    vmem = pl.BlockSpec(memory_space=pltpu.VMEM)
    smem = pl.BlockSpec(memory_space=pltpu.SMEM)
    send, lim = pl.pallas_call(
        functools.partial(pick_kernel, peers),
        out_shape=(
            jax.ShapeDtypeStruct((peers, count, 2, piece_keys, hd), cluster_kv.dtype),
            jax.ShapeDtypeStruct((peers, count), jnp.int32),
        ),
        in_specs=[smem, smem, smem, pl.BlockSpec(memory_space=pl.ANY)],
        out_specs=(vmem, smem),
        scratch_shapes=[
            pltpu.SMEM((pieces + 1,), jnp.int32),
            pltpu.SMEM((peers,), jnp.int32),
            pltpu.SemaphoreType.DMA,
        ],
        name="pick",
    )(cluster_ids[:, 0, :], piece_slot, cluster_len, cluster_kv)
    rows = heads * tok
    any_space = pl.BlockSpec(memory_space=pl.ANY)
    attended, w_pair = pl.pallas_call(
        functools.partial(attend_kernel, peers, heads),
        out_shape=(
            jax.ShapeDtypeStruct((tok, heads * hd), jnp.bfloat16),
            jax.ShapeDtypeStruct(w_out.shape, w_out.dtype),
        ),
        in_specs=[smem, vmem, vmem, vmem, vmem, any_space],
        out_specs=(vmem, any_space),
        scratch_shapes=[
            pltpu.VMEM((peers, count, 2, piece_keys, hd), cluster_kv.dtype),
            pltpu.VMEM((hd, rows), jnp.bfloat16),
            pltpu.VMEM((hd, count * piece_keys), jnp.bfloat16),
            pltpu.VMEM((1, rows), jnp.float32),
            pltpu.VMEM((1, rows), jnp.float32),
            pltpu.VMEM((hd, rows), jnp.float32),
            pltpu.SemaphoreType.DMA((peers,)),
            pltpu.SemaphoreType.DMA((peers,)),
            pltpu.SemaphoreType.DMA((2,)),
        ],
        compiler_params=pltpu.CompilerParams(
            collective_id=0, has_side_effects=True, vmem_limit_bytes=40 * 2**20),
        name="attend",
    )(lim, send, queries.reshape(tok, heads * hd), new_keys[:, 0], new_values[:, 0], w_out)
    far = peers // 2
    half = tok // lax.axis_size("head")
    depth, columns = w_out.shape
    return pl.pallas_call(
        functools.partial(project_kernel, far),
        out_shape=jax.ShapeDtypeStruct((half, peers * columns), jnp.bfloat16),
        in_specs=[any_space, any_space, any_space],
        out_specs=vmem,
        scratch_shapes=[
            pltpu.VMEM((far, tok, depth), jnp.bfloat16),
            pltpu.VMEM((2, depth, columns), w_out.dtype),
            pltpu.VMEM((far, 2, half, 2 * columns), jnp.float32),
            pltpu.VMEM((far, half, 2 * columns), jnp.float32),
            pltpu.VMEM((far, half, 2 * columns), jnp.bfloat16),
            pltpu.SemaphoreType.DMA((3,)),
            pltpu.SemaphoreType.DMA((2, far)),
            pltpu.SemaphoreType.DMA((far,)),
            pltpu.SemaphoreType.DMA((far,)),
            pltpu.SemaphoreType.DMA((far,)),
            pltpu.SemaphoreType.DMA((far,)),
            pltpu.SemaphoreType.DMA((far,)),
        ],
        compiler_params=pltpu.CompilerParams(
            collective_id=1, has_side_effects=True, vmem_limit_bytes=40 * 2**20),
        name="project",
    )(attended, w_out, w_pair)


def solution(mesh):
    return jax.shard_map(
        local,
        mesh=mesh,
        in_specs=(
            P(("groups", "req"), "head", None),
            P(("groups", "req"), "head", None),
            P(("groups", "req"), "head", None),
            P(("groups", "req"), "head", None, None, None),
            P("groups"),
            P("groups", None),
            P("groups", "head", None),
            P("head", "req"),
        ),
        out_specs=P(("groups", "req", "head"), None),
        check_vma=False,
    )
```

```python
import functools

import jax
import jax.numpy as jnp
from jax import lax
from jax.experimental import pallas as pl
from jax.experimental.pallas import tpu as pltpu
from jax.sharding import PartitionSpec as P

MESH = pl.DeviceIdType.MESH
NEG = -1e30
LOG2E = 1.4426950408889634


def pick_kernel(peers, ids_ref, slot_ref, len_ref, kv_ref, send_ref, lim_ref, pick, count, sem):
    me = lax.axis_index("req")
    held, _, _, piece_keys, _ = kv_ref.shape
    sel = ids_ref.shape[1]
    pieces = slot_ref.shape[1]
    per = pieces // peers
    base = me * held

    @pl.loop(0, peers)
    def _(r):
        for s in range(sel):
            c = ids_ref[r, s]
            n = jnp.int32(0)
            for p in range(pieces):
                loc = slot_ref[c, p] - base
                pick[n] = loc
                n = n + ((loc >= 0) & (loc < held)).astype(jnp.int32)
            for j in range(per):
                pltpu.make_async_copy(kv_ref.at[pick[j], 0], send_ref.at[r, s * per + j], sem).start()

    for s in range(sel):
        c = ids_ref[me, s]
        fill = len_ref[c]
        for o in range(peers):
            count[o] = 0
        for p in range(pieces):
            o = slot_ref[c, p] // held
            j = count[o]
            lim_ref[o, s * per + j] = fill - p * piece_keys
            count[o] = j + 1
    pltpu.make_async_copy(send_ref, send_ref, sem).wait()


def attend_kernel(peers, heads, lim_ref, send_ref, q_ref, k_ref, v_ref, w_ref, out_ref, w_pair_ref,
                  recv, qt, top, total, acc, send_sem, recv_sem, w_sem):
    me = lax.axis_index("req")
    tok = q_ref.shape[0]
    hd = k_ref.shape[1]
    count = send_ref.shape[1]
    piece_keys = send_ref.shape[3]
    rows = heads * tok
    block = min(128, rows)
    phases = send_sem.shape[1]
    group = count // phases
    factor = hd ** (-0.5) * LOG2E

    barrier = pltpu.get_barrier_semaphore()
    for k in range(1, peers):
        pl.semaphore_signal(barrier, inc=1, device_id={"req": lax.rem(me + k, peers)}, device_id_type=MESH)
    pl.semaphore_wait(barrier, peers - 1)

    def peer_of(i):
        off = jnp.where(i % 2 == 1, (i + 1) // 2, peers - i // 2)
        return lax.rem(me + off, peers)

    def copy_to(peer, f):
        part = pl.ds(f * group, group)
        return pltpu.make_async_remote_copy(
            src_ref=send_ref.at[peer, part], dst_ref=recv.at[me, part],
            send_sem=send_sem.at[peer, f], recv_sem=recv_sem.at[me, f],
            device_id={"req": peer}, device_id_type=MESH)

    def copy_from(peer, f):
        part = pl.ds(f * group, group)
        return pltpu.make_async_remote_copy(
            src_ref=send_ref.at[peer, part], dst_ref=recv.at[peer, part],
            send_sem=send_sem.at[peer, f], recv_sem=recv_sem.at[peer, f],
            device_id={"req": peer}, device_id_type=MESH)

    @pl.loop(0, phases)
    def _(f):
        @pl.loop(1, peers)
        def _(i):
            copy_to(peer_of(i), f).start()

    pair_copy = pltpu.make_async_remote_copy(
        src_ref=w_ref, dst_ref=w_pair_ref, send_sem=w_sem.at[0], recv_sem=w_sem.at[1],
        device_id={"req": me + 1 - 2 * (me % 2)}, device_id_type=MESH)
    pair_copy.start()

    for h in range(heads):
        cols = slice(h * hd, (h + 1) * hd)
        qt[:, h * tok:(h + 1) * tok] = q_ref[:, cols].T
    own_vt = v_ref[...].T

    @pl.loop(0, rows // block)
    def _(b):
        cols = pl.ds(pl.multiple_of(b * block, block), block)
        s = jnp.dot(k_ref[...], qt[:, cols], preferred_element_type=jnp.float32)
        u = lax.broadcasted_iota(jnp.int32, s.shape, 0)
        t = lax.broadcasted_iota(jnp.int32, s.shape, 1) % tok
        s = jnp.where(u <= t, s, NEG)
        m = jnp.max(s, axis=0, keepdims=True)
        w = jnp.exp2((s - m) * factor)
        top[:, cols] = m
        total[:, cols] = jnp.sum(w, axis=0, keepdims=True)
        acc[:, cols] = jnp.dot(own_vt, w.astype(jnp.bfloat16), preferred_element_type=jnp.float32)

    def attend(src_ref, peer, f):
        keys = group * piece_keys
        k = src_ref[peer, pl.ds(f * group, group), 0].reshape(keys, hd)
        vt = jnp.concatenate([src_ref[peer, f * group + i, 1].T for i in range(group)], axis=1)
        fills = [lim_ref[peer, f * group + i] for i in range(group)]
        key = lax.broadcasted_iota(jnp.int32, (piece_keys, block), 0)

        def score(b):
            s = jnp.dot(k, qt[:, b * block:(b + 1) * block], preferred_element_type=jnp.float32)
            return jnp.concatenate(
                [jnp.where(key < fills[i], s[i * piece_keys:(i + 1) * piece_keys], NEG) for i in range(group)], axis=0)

        def weigh(b, s):
            cols = slice(b * block, (b + 1) * block)
            m_old = top[:, cols]
            m = jnp.maximum(m_old, jnp.max(s, axis=0, keepdims=True))
            keep = jnp.exp2((m_old - m) * factor)
            w = jnp.exp2((s - m) * factor)
            mixed = jnp.dot(vt, w.astype(jnp.bfloat16), preferred_element_type=jnp.float32)
            top[:, cols] = m
            total[:, cols] = total[:, cols] * keep + jnp.sum(w, axis=0, keepdims=True)
            acc[:, cols] = acc[:, cols] * keep + mixed

        s = score(0)
        for b in range(rows // block):
            ahead = score(b + 1) if b + 1 < rows // block else None
            weigh(b, s)
            s = ahead

    @pl.loop(0, phases)
    def _(f):
        attend(send_ref, me, f)

    @pl.loop(0, phases * (peers - 1))
    def _(step):
        f = step // (peers - 1)
        peer = peer_of(step % (peers - 1) + 1)
        copy_from(peer, f).wait_recv()
        attend(recv, peer, f)

    for h in range(heads):
        rows_h = slice(h * tok, (h + 1) * tok)
        o = acc[:, rows_h] / total[:, rows_h]
        out_ref[:, h * hd:(h + 1) * hd] = o.T.astype(out_ref.dtype)

    @pl.loop(0, phases)
    def _(f):
        @pl.loop(1, peers)
        def _(i):
            copy_to(peer_of(i), f).wait_send()

    pair_copy.wait()


def project_kernel(far, att_ref, w_ref, w_pair_ref, out_ref,
                   full, wv, part, got, low, load_sem, send_sem, recv_sem,
                   part_send, part_recv, out_send, out_recv):
    me = lax.axis_index("req")
    head = lax.axis_index("head")
    hi, lo = me // 2, me % 2
    half = out_ref.shape[0]
    columns = w_ref.shape[1]
    wide = 2 * columns

    def at(z):
        return {"req": z * 2 + lo}

    load_own = pltpu.make_async_copy(att_ref, full.at[hi], load_sem.at[0])
    load_w = pltpu.make_async_copy(w_ref, wv.at[lo], load_sem.at[1])
    load_pair = pltpu.make_async_copy(w_pair_ref, wv.at[1 - lo], load_sem.at[2])
    load_own.start()
    load_w.start()
    load_pair.start()

    barrier = pltpu.get_barrier_semaphore()
    for k in range(1, far):
        pl.semaphore_signal(barrier, inc=1, device_id=at(lax.rem(hi + k, far)), device_id_type=MESH)
    pl.semaphore_signal(barrier, inc=1, device_id={"head": 1 - head}, device_id_type=MESH)
    pl.semaphore_wait(barrier, far)

    def block_copy(z, to, way):
        return pltpu.make_async_remote_copy(
            src_ref=full.at[z], dst_ref=full.at[z], send_sem=send_sem.at[way, z],
            recv_sem=recv_sem.at[z], device_id=at(to), device_id_type=MESH)

    def part_copy(z):
        return pltpu.make_async_remote_copy(
            src_ref=part.at[z, 1 - head], dst_ref=got.at[z], send_sem=part_send.at[z],
            recv_sem=part_recv.at[z], device_id={"head": 1 - head}, device_id_type=MESH)

    def out_copy(z, owner):
        return pltpu.make_async_remote_copy(
            src_ref=low.at[z], dst_ref=out_ref.at[:, pl.ds(pl.multiple_of(owner * wide, wide), wide)],
            send_sem=out_send.at[z], recv_sem=out_recv.at[owner], device_id=at(z), device_id_type=MESH)

    def compute(z):
        @pl.loop(0, 2)
        def _(j):
            cols = pl.ds(pl.multiple_of(j * columns, columns), columns)
            terms = jnp.dot(full[z], wv[j], preferred_element_type=jnp.float32)
            part[z, 0, :, cols] = terms[:half]
            part[z, 1, :, cols] = terms[half:]
        part_copy(z).start()

    def finish(z):
        part_copy(z).wait_recv()
        rows = (part[z, head] + got[z]).astype(out_ref.dtype)

        @pl.when(z == hi)
        def _():
            out_ref[:, pl.ds(pl.multiple_of(hi * wide, wide), wide)] = rows

        @pl.when(z != hi)
        def _():
            low[z] = rows
            out_copy(z, hi).start()

    load_own.wait()

    @pl.when(hi < far - 1)
    def _():
        block_copy(hi, hi + 1, 0).start()

    @pl.when(hi > 0)
    def _():
        block_copy(hi, hi - 1, 1).start()

    load_w.wait()
    load_pair.wait()
    compute(hi)

    @pl.loop(1, far + 1)
    def _(d):
        @pl.when((hi - d >= 0) & (d < far))
        def _():
            block_copy(hi - d, hi, 0).wait_recv()

            @pl.when(hi < far - 1)
            def _():
                block_copy(hi - d, hi + 1, 0).start()

        @pl.when(hi + d < far)
        def _():
            block_copy(hi + d, hi, 1).wait_recv()

            @pl.when(hi > 0)
            def _():
                block_copy(hi + d, hi - 1, 1).start()

        @pl.loop(0, 2)
        def _(side):
            z = hi + d * (2 * side - 1)

            @pl.when((z >= 0) & (z < far))
            def _():
                compute(z)

        @pl.loop(0, 2)
        def _(side):
            z = hi + (d - 1) * (2 * side - 1)

            @pl.when((z >= 0) & (z < far) & ((d > 1) | (side == 0)))
            def _():
                finish(z)

    @pl.loop(0, far)
    def _(z):
        @pl.when((z <= hi) & (hi < far - 1))
        def _():
            block_copy(z, hi + 1, 0).wait_send()

        @pl.when((z >= hi) & (hi > 0))
        def _():
            block_copy(z, hi - 1, 1).wait_send()

        part_copy(z).wait_send()

        @pl.when(z != hi)
        def _():
            out_copy(z, hi).wait_send()
            out_copy(z, z).wait_recv()


def local(queries, new_keys, new_values, cluster_kv, cluster_len, piece_slot, cluster_ids, w_out):
    peers = lax.axis_size("req")
    tok, heads, hd = queries.shape
    piece_keys = cluster_kv.shape[3]
    pieces = piece_slot.shape[1]
    sel = cluster_ids.shape[2]
    count = sel * (pieces // peers)
    vmem = pl.BlockSpec(memory_space=pltpu.VMEM)
    smem = pl.BlockSpec(memory_space=pltpu.SMEM)
    send, lim = pl.pallas_call(
        functools.partial(pick_kernel, peers),
        out_shape=(
            jax.ShapeDtypeStruct((peers, count, 2, piece_keys, hd), cluster_kv.dtype),
            jax.ShapeDtypeStruct((peers, count), jnp.int32),
        ),
        in_specs=[smem, smem, smem, pl.BlockSpec(memory_space=pl.ANY)],
        out_specs=(vmem, smem),
        scratch_shapes=[
            pltpu.SMEM((pieces + 1,), jnp.int32),
            pltpu.SMEM((peers,), jnp.int32),
            pltpu.SemaphoreType.DMA,
        ],
        name="pick",
    )(cluster_ids[:, 0, :], piece_slot, cluster_len, cluster_kv)
    rows = heads * tok
    phases = min(4, count)
    any_space = pl.BlockSpec(memory_space=pl.ANY)
    attended, w_pair = pl.pallas_call(
        functools.partial(attend_kernel, peers, heads),
        out_shape=(
            jax.ShapeDtypeStruct((tok, heads * hd), jnp.bfloat16),
            jax.ShapeDtypeStruct(w_out.shape, w_out.dtype),
        ),
        in_specs=[smem, vmem, vmem, vmem, vmem, any_space],
        out_specs=(vmem, any_space),
        scratch_shapes=[
            pltpu.VMEM((peers, count, 2, piece_keys, hd), cluster_kv.dtype),
            pltpu.VMEM((hd, rows), jnp.bfloat16),
            pltpu.VMEM((1, rows), jnp.float32),
            pltpu.VMEM((1, rows), jnp.float32),
            pltpu.VMEM((hd, rows), jnp.float32),
            pltpu.SemaphoreType.DMA((peers, phases)),
            pltpu.SemaphoreType.DMA((peers, phases)),
            pltpu.SemaphoreType.DMA((2,)),
        ],
        compiler_params=pltpu.CompilerParams(
            collective_id=0, has_side_effects=True, vmem_limit_bytes=40 * 2**20),
        name="attend",
    )(lim, send, queries.reshape(tok, heads * hd), new_keys[:, 0], new_values[:, 0], w_out)
    far = peers // 2
    half = tok // lax.axis_size("head")
    depth, columns = w_out.shape
    return pl.pallas_call(
        functools.partial(project_kernel, far),
        out_shape=jax.ShapeDtypeStruct((half, peers * columns), jnp.bfloat16),
        in_specs=[any_space, any_space, any_space],
        out_specs=vmem,
        scratch_shapes=[
            pltpu.VMEM((far, tok, depth), jnp.bfloat16),
            pltpu.VMEM((2, depth, columns), w_out.dtype),
            pltpu.VMEM((far, 2, half, 2 * columns), jnp.float32),
            pltpu.VMEM((far, half, 2 * columns), jnp.float32),
            pltpu.VMEM((far, half, 2 * columns), jnp.bfloat16),
            pltpu.SemaphoreType.DMA((3,)),
            pltpu.SemaphoreType.DMA((2, far)),
            pltpu.SemaphoreType.DMA((far,)),
            pltpu.SemaphoreType.DMA((far,)),
            pltpu.SemaphoreType.DMA((far,)),
            pltpu.SemaphoreType.DMA((far,)),
            pltpu.SemaphoreType.DMA((far,)),
        ],
        compiler_params=pltpu.CompilerParams(
            collective_id=1, has_side_effects=True, vmem_limit_bytes=40 * 2**20),
        name="project",
    )(attended, w_out, w_pair)


def solution(mesh):
    return jax.shard_map(
        local,
        mesh=mesh,
        in_specs=(
            P(("groups", "req"), "head", None),
            P(("groups", "req"), "head", None),
            P(("groups", "req"), "head", None),
            P(("groups", "req"), "head", None, None, None),
            P("groups"),
            P("groups", None),
            P("groups", "head", None),
            P("head", "req"),
        ),
        out_specs=P(("groups", "req", "head"), None),
        check_vma=False,
    )
```

```python
import functools

import jax
import jax.numpy as jnp
from jax import lax
from jax.experimental import pallas as pl
from jax.experimental.pallas import tpu as pltpu
from jax.sharding import PartitionSpec as P

MESH = pl.DeviceIdType.MESH
NEG = -1e30
LOG2E = 1.4426950408889634


def pick_kernel(peers, ids_ref, slot_ref, len_ref, kv_ref, send_ref, lim_ref, pick, count, held_pieces, in_sem, out_sem):
    me = lax.axis_index("req")
    held, _, _, piece_keys, _ = kv_ref.shape
    sel = ids_ref.shape[2]
    pieces = slot_ref.shape[1]
    per = pieces // peers
    base = me * held

    @pl.loop(0, peers)
    def _(r):
        for s in range(sel):
            c = ids_ref[r, 0, s]
            n = jnp.int32(0)
            for p in range(pieces):
                loc = slot_ref[c, p] - base
                pick[n] = loc
                n = n + ((loc >= 0) & (loc < held)).astype(jnp.int32)
            for j in range(per):
                pltpu.make_async_copy(kv_ref.at[pick[j], 0], held_pieces.at[r, s * per + j], in_sem.at[r]).start()

    for s in range(sel):
        c = ids_ref[me, 0, s]
        fill = len_ref[c]
        for o in range(peers):
            count[o] = 0
        for p in range(pieces):
            o = slot_ref[c, p] // held
            j = count[o]
            lim_ref[o, s * per + j] = fill - p * piece_keys
            count[o] = j + 1

    def put(r):
        return pltpu.make_async_copy(held_pieces.at[r], send_ref.at[r], out_sem.at[r])

    @pl.loop(0, peers)
    def _(r):
        pltpu.make_async_copy(send_ref.at[r], held_pieces.at[r], in_sem.at[r]).wait()
        put(r).start()

    @pl.loop(0, peers)
    def _(r):
        put(r).wait()


def attend_kernel(peers, heads, lim_ref, send_ref, q_ref, k_ref, v_ref, w_ref, out_ref, w_pair_ref,
                  recv, qt, top, total, acc, send_sem, recv_sem, w_sem, own_sem):
    me = lax.axis_index("req")
    tok = q_ref.shape[0]
    hd = k_ref.shape[1]
    count = send_ref.shape[1]
    piece_keys = send_ref.shape[3]
    rows = heads * tok
    block = min(128, rows)
    phases = send_sem.shape[1]
    group = count // phases
    factor = hd ** (-0.5) * LOG2E

    own_copy = pltpu.make_async_copy(send_ref.at[me], recv.at[me], own_sem)
    own_copy.start()
    barrier = pltpu.get_barrier_semaphore()
    for k in range(1, peers):
        pl.semaphore_signal(barrier, inc=1, device_id={"req": lax.rem(me + k, peers)}, device_id_type=MESH)
    pl.semaphore_wait(barrier, peers - 1)

    def peer_of(i):
        off = jnp.where(i % 2 == 1, (i + 1) // 2, peers - i // 2)
        return lax.rem(me + off, peers)

    def copy_to(peer, f):
        part = pl.ds(f * group, group)
        return pltpu.make_async_remote_copy(
            src_ref=send_ref.at[peer, part], dst_ref=recv.at[me, part],
            send_sem=send_sem.at[peer, f], recv_sem=recv_sem.at[me, f],
            device_id={"req": peer}, device_id_type=MESH)

    def copy_from(peer, f):
        part = pl.ds(f * group, group)
        return pltpu.make_async_remote_copy(
            src_ref=send_ref.at[peer, part], dst_ref=recv.at[peer, part],
            send_sem=send_sem.at[peer, f], recv_sem=recv_sem.at[peer, f],
            device_id={"req": peer}, device_id_type=MESH)

    @pl.loop(0, phases)
    def _(f):
        @pl.loop(1, peers)
        def _(i):
            copy_to(peer_of(i), f).start()

    pair_copy = pltpu.make_async_remote_copy(
        src_ref=w_ref, dst_ref=w_pair_ref, send_sem=w_sem.at[0], recv_sem=w_sem.at[1],
        device_id={"req": me + 1 - 2 * (me % 2)}, device_id_type=MESH)
    pair_copy.start()

    for h in range(heads):
        qt[:, h * tok:(h + 1) * tok] = q_ref[:, h, :].T
    own_vt = v_ref[...].T

    @pl.loop(0, rows // block)
    def _(b):
        cols = pl.ds(pl.multiple_of(b * block, block), block)
        s = jnp.dot(k_ref[...], qt[:, cols], preferred_element_type=jnp.float32)
        u = lax.broadcasted_iota(jnp.int32, s.shape, 0)
        t = lax.broadcasted_iota(jnp.int32, s.shape, 1) % tok
        s = jnp.where(u <= t, s, NEG)
        m = jnp.max(s, axis=0, keepdims=True)
        w = jnp.exp2((s - m) * factor)
        top[:, cols] = m
        total[:, cols] = jnp.sum(w, axis=0, keepdims=True)
        acc[:, cols] = jnp.dot(own_vt, w.astype(jnp.bfloat16), preferred_element_type=jnp.float32)

    def attend(src_ref, peer, f):
        keys = group * piece_keys
        k = src_ref[peer, pl.ds(f * group, group), 0].reshape(keys, hd)
        vt = jnp.concatenate([src_ref[peer, f * group + i, 1].T for i in range(group)], axis=1)
        fills = [lim_ref[peer, f * group + i] for i in range(group)]
        key = lax.broadcasted_iota(jnp.int32, (piece_keys, block), 0)

        def score(b):
            s = jnp.dot(k, qt[:, b * block:(b + 1) * block], preferred_element_type=jnp.float32)
            return jnp.concatenate(
                [jnp.where(key < fills[i], s[i * piece_keys:(i + 1) * piece_keys], NEG) for i in range(group)], axis=0)

        def weigh(b, s):
            cols = slice(b * block, (b + 1) * block)
            m_old = top[:, cols]
            m = jnp.maximum(m_old, jnp.max(s, axis=0, keepdims=True))
            keep = jnp.exp2((m_old - m) * factor)
            w = jnp.exp2((s - m) * factor)
            mixed = jnp.dot(vt, w.astype(jnp.bfloat16), preferred_element_type=jnp.float32)
            top[:, cols] = m
            total[:, cols] = total[:, cols] * keep + jnp.sum(w, axis=0, keepdims=True)
            acc[:, cols] = acc[:, cols] * keep + mixed

        s = score(0)
        for b in range(rows // block):
            ahead = score(b + 1) if b + 1 < rows // block else None
            weigh(b, s)
            s = ahead

    own_copy.wait()

    @pl.loop(0, phases)
    def _(f):
        attend(recv, me, f)

    @pl.loop(0, phases * (peers - 1))
    def _(step):
        f = step // (peers - 1)
        peer = peer_of(step % (peers - 1) + 1)
        copy_from(peer, f).wait_recv()
        attend(recv, peer, f)

    for h in range(heads):
        rows_h = slice(h * tok, (h + 1) * tok)
        o = acc[:, rows_h] / total[:, rows_h]
        out_ref[:, h * hd:(h + 1) * hd] = o.T.astype(out_ref.dtype)

    @pl.loop(0, phases)
    def _(f):
        @pl.loop(1, peers)
        def _(i):
            copy_to(peer_of(i), f).wait_send()

    pair_copy.wait()


def project_kernel(far, att_ref, w_ref, w_pair_ref, out_ref,
                   full, wv, part, got, low, load_sem, send_sem, recv_sem,
                   part_send, part_recv, out_send, out_recv):
    me = lax.axis_index("req")
    head = lax.axis_index("head")
    hi, lo = me // 2, me % 2
    half = out_ref.shape[0]
    columns = w_ref.shape[1]
    wide = 2 * columns

    def at(z):
        return {"req": z * 2 + lo}

    load_own = pltpu.make_async_copy(att_ref, full.at[hi], load_sem.at[0])
    load_w = pltpu.make_async_copy(w_ref, wv.at[lo], load_sem.at[1])
    load_pair = pltpu.make_async_copy(w_pair_ref, wv.at[1 - lo], load_sem.at[2])
    load_own.start()
    load_w.start()
    load_pair.start()

    barrier = pltpu.get_barrier_semaphore()
    for k in range(1, far):
        pl.semaphore_signal(barrier, inc=1, device_id=at(lax.rem(hi + k, far)), device_id_type=MESH)
    pl.semaphore_signal(barrier, inc=1, device_id={"head": 1 - head}, device_id_type=MESH)
    pl.semaphore_wait(barrier, far)

    def block_copy(z, to, way):
        return pltpu.make_async_remote_copy(
            src_ref=full.at[z], dst_ref=full.at[z], send_sem=send_sem.at[way, z],
            recv_sem=recv_sem.at[z], device_id=at(to), device_id_type=MESH)

    def part_copy(z):
        return pltpu.make_async_remote_copy(
            src_ref=part.at[z, 1 - head], dst_ref=got.at[z], send_sem=part_send.at[z],
            recv_sem=part_recv.at[z], device_id={"head": 1 - head}, device_id_type=MESH)

    def out_copy(z, owner):
        return pltpu.make_async_remote_copy(
            src_ref=low.at[z], dst_ref=out_ref.at[:, pl.ds(pl.multiple_of(owner * wide, wide), wide)],
            send_sem=out_send.at[z], recv_sem=out_recv.at[owner], device_id=at(z), device_id_type=MESH)

    def compute(z):
        @pl.loop(0, 2)
        def _(j):
            cols = pl.ds(pl.multiple_of(j * columns, columns), columns)
            terms = jnp.dot(full[z], wv[j], preferred_element_type=jnp.float32)
            part[z, 0, :, cols] = terms[:half]
            part[z, 1, :, cols] = terms[half:]
        part_copy(z).start()

    def finish(z):
        part_copy(z).wait_recv()
        rows = (part[z, head] + got[z]).astype(out_ref.dtype)

        @pl.when(z == hi)
        def _():
            out_ref[:, pl.ds(pl.multiple_of(hi * wide, wide), wide)] = rows

        @pl.when(z != hi)
        def _():
            low[z] = rows
            out_copy(z, hi).start()

    load_own.wait()

    @pl.when(hi < far - 1)
    def _():
        block_copy(hi, hi + 1, 0).start()

    @pl.when(hi > 0)
    def _():
        block_copy(hi, hi - 1, 1).start()

    load_w.wait()
    load_pair.wait()
    compute(hi)

    @pl.loop(1, far + 1)
    def _(d):
        @pl.when((hi - d >= 0) & (d < far))
        def _():
            block_copy(hi - d, hi, 0).wait_recv()

            @pl.when(hi < far - 1)
            def _():
                block_copy(hi - d, hi + 1, 0).start()

        @pl.when(hi + d < far)
        def _():
            block_copy(hi + d, hi, 1).wait_recv()

            @pl.when(hi > 0)
            def _():
                block_copy(hi + d, hi - 1, 1).start()

        @pl.loop(0, 2)
        def _(side):
            z = hi + d * (2 * side - 1)

            @pl.when((z >= 0) & (z < far))
            def _():
                compute(z)

        @pl.loop(0, 2)
        def _(side):
            z = hi + (d - 1) * (2 * side - 1)

            @pl.when((z >= 0) & (z < far) & ((d > 1) | (side == 0)))
            def _():
                finish(z)

    @pl.loop(0, far)
    def _(z):
        @pl.when((z <= hi) & (hi < far - 1))
        def _():
            block_copy(z, hi + 1, 0).wait_send()

        @pl.when((z >= hi) & (hi > 0))
        def _():
            block_copy(z, hi - 1, 1).wait_send()

        part_copy(z).wait_send()

        @pl.when(z != hi)
        def _():
            out_copy(z, hi).wait_send()
            out_copy(z, z).wait_recv()


def local(queries, new_keys, new_values, cluster_kv, cluster_len, piece_slot, cluster_ids, w_out):
    peers = lax.axis_size("req")
    tok, heads, hd = queries.shape
    piece_keys = cluster_kv.shape[3]
    pieces = piece_slot.shape[1]
    sel = cluster_ids.shape[2]
    count = sel * (pieces // peers)
    vmem = pl.BlockSpec(memory_space=pltpu.VMEM)
    smem = pl.BlockSpec(memory_space=pltpu.SMEM)
    any_space = pl.BlockSpec(memory_space=pltpu.HBM)
    send, lim = pl.pallas_call(
        functools.partial(pick_kernel, peers),
        out_shape=(
            jax.ShapeDtypeStruct((peers, count, 2, piece_keys, hd), cluster_kv.dtype),
            jax.ShapeDtypeStruct((peers, count), jnp.int32),
        ),
        in_specs=[smem, smem, smem, any_space],
        out_specs=(any_space, smem),
        scratch_shapes=[
            pltpu.SMEM((pieces + 1,), jnp.int32),
            pltpu.SMEM((peers,), jnp.int32),
            pltpu.VMEM((peers, count, 2, piece_keys, hd), cluster_kv.dtype),
            pltpu.SemaphoreType.DMA((peers,)),
            pltpu.SemaphoreType.DMA((peers,)),
        ],
        name="pick",
    )(cluster_ids, piece_slot, cluster_len, cluster_kv)
    rows = heads * tok
    phases = min(4, count)
    attended, w_pair = pl.pallas_call(
        functools.partial(attend_kernel, peers, heads),
        out_shape=(
            jax.ShapeDtypeStruct((tok, heads * hd), jnp.bfloat16),
            jax.ShapeDtypeStruct(w_out.shape, w_out.dtype),
        ),
        in_specs=[smem, any_space, vmem, vmem, vmem, any_space],
        out_specs=(vmem, any_space),
        scratch_shapes=[
            pltpu.VMEM((peers, count, 2, piece_keys, hd), cluster_kv.dtype),
            pltpu.VMEM((hd, rows), jnp.bfloat16),
            pltpu.VMEM((1, rows), jnp.float32),
            pltpu.VMEM((1, rows), jnp.float32),
            pltpu.VMEM((hd, rows), jnp.float32),
            pltpu.SemaphoreType.DMA((peers, phases)),
            pltpu.SemaphoreType.DMA((peers, phases)),
            pltpu.SemaphoreType.DMA((2,)),
            pltpu.SemaphoreType.DMA,
        ],
        compiler_params=pltpu.CompilerParams(
            collective_id=0, has_side_effects=True, vmem_limit_bytes=60 * 2**20),
        name="attend",
    )(lim, send, queries, new_keys[:, 0], new_values[:, 0], w_out)
    far = peers // 2
    half = tok // lax.axis_size("head")
    depth, columns = w_out.shape
    return pl.pallas_call(
        functools.partial(project_kernel, far),
        out_shape=jax.ShapeDtypeStruct((half, peers * columns), jnp.bfloat16),
        in_specs=[any_space, any_space, any_space],
        out_specs=vmem,
        scratch_shapes=[
            pltpu.VMEM((far, tok, depth), jnp.bfloat16),
            pltpu.VMEM((2, depth, columns), w_out.dtype),
            pltpu.VMEM((far, 2, half, 2 * columns), jnp.float32),
            pltpu.VMEM((far, half, 2 * columns), jnp.float32),
            pltpu.VMEM((far, half, 2 * columns), jnp.bfloat16),
            pltpu.SemaphoreType.DMA((3,)),
            pltpu.SemaphoreType.DMA((2, far)),
            pltpu.SemaphoreType.DMA((far,)),
            pltpu.SemaphoreType.DMA((far,)),
            pltpu.SemaphoreType.DMA((far,)),
            pltpu.SemaphoreType.DMA((far,)),
            pltpu.SemaphoreType.DMA((far,)),
        ],
        compiler_params=pltpu.CompilerParams(
            collective_id=1, has_side_effects=True, vmem_limit_bytes=60 * 2**20),
        name="project",
    )(attended, w_out, w_pair)


def solution(mesh):
    return jax.shard_map(
        local,
        mesh=mesh,
        in_specs=(
            P(("groups", "req"), "head", None),
            P(("groups", "req"), "head", None),
            P(("groups", "req"), "head", None),
            P(("groups", "req"), "head", None, None, None),
            P("groups"),
            P("groups", None),
            P("groups", "head", None),
            P("head", "req"),
        ),
        out_specs=P(("groups", "req", "head"), None),
        check_vma=False,
    )
```
